32 devices in a mesh: dp: 4 (over y, x), px: 4 (over z), py: 2 (over core).
Axes of the slice: x: 2, y: 2, z: 4, core: 2. Of those that a mesh axis runs over, the one named last changes fastest.
Arguments:
- fields: bfloat16 [4, 16, 16, 32, 256], P('dp', 'px', 'py'), may hold values from -6 to 6
- cotangent: bfloat16 [4, 16, 16, 32, 256], P('dp', 'px', 'py'), may hold values from -6 to 6
- first_weight: bfloat16 [6912, 256], replicated, may hold values from -0.078125 to 0.078125
- second_weight: bfloat16 [6912, 256], replicated, may hold values from -0.078125 to 0.078125
Outputs:
- output: bfloat16 [4, 16, 16, 32, 256], P('dp', 'px', 'py')
- field_grad: bfloat16 [4, 16, 16, 32, 256], P('dp', 'px', 'py')
- first_grad: float32 [6912, 256], P('dp', ('px', 'py'))
- second_grad: float32 [6912, 256], P('dp', ('px', 'py'))
The draws below stay inside these ranges and needn't reach their ends.
All inputs are finite; a program needn't handle non-finite values.
Results may differ from the reference program's by a relative error of at most 0.0033.
Values may be sent and summed in bfloat16 or wider, within the bound.
A program may use at most 128 MiB of HBM per device.

```python
import jax
import jax.numpy as jnp
from jax import lax

C = 256
KC = 6912
ROLL = 4
NX = 16
NY = 16
NZ = 32


def shard_levels(stream_key, shape, shards, low, top_value):
    factor_of, own = 1.0, jax.random.fold_in(stream_key, 6)
    for dim, blocks in shards:
        draws = jnp.exp(jax.random.uniform(jax.random.fold_in(own, dim), (blocks,), jnp.float32, low / len(shards), top_value / len(shards)))
        factor_of = factor_of * jnp.repeat(draws, shape[dim] // blocks).reshape([-1 if axis == dim else 1 for axis in range(len(shape))])
    return factor_of


def centred(rng, dims, scale, most, split=(), dtype=jnp.bfloat16):
    loudness = shard_levels(rng, dims, split, -0.22, 0.18) if split else 1.0
    drawn = jax.random.normal(rng, dims, jnp.float32) * scale * loudness
    return jnp.minimum(jnp.maximum(drawn, -most), most).astype(dtype)


def setup_inputs(seed: int = 0) -> dict:
    key_of = jax.random.split(jax.random.key(seed), 5)
    return {
        "fields": centred(key_of[0], (ROLL, NX, NY, NZ, C), 1.0, 6.0, ((0, 4), (1, 4), (2, 2))),
        "cotangent": centred(key_of[1], (ROLL, NX, NY, NZ, C), 1.0, 6.0, ((0, 4), (1, 4), (2, 2))),
        "first_weight": centred(key_of[2], (KC, C), KC ** -0.5, 0.078125),
        "second_weight": centred(key_of[3], (KC, C), KC ** -0.5, 0.078125),
    }


def gelu_tanh(v):
    return jax.nn.gelu(v, approximate=True)

def padded_grid(field):
    return jnp.pad(field, ((1, 1), (1, 1), (1, 1), (0, 0)))

def window(padded, start_x, start_y, start_z):
    size_x, size_y, size_z, width = padded.shape
    block = padded[start_x:start_x + size_x - 2, start_y:start_y + size_y - 2, start_z:start_z + size_z - 2, :]
    return block.reshape(-1, width)

def conv_forward(padded, weight):
    width = padded.shape[-1]
    total = None
    for offset in range(27):
        first, second, third = (offset // 9, offset // 3 % 3, offset % 3)
        block = weight[offset * width:(offset + 1) * width]
        term = jnp.dot(window(padded, first, second, third), block, preferred_element_type=jnp.float32)
        total = term if total is None else total + term
    return total

def conv_transposed(padded, weight):
    width = padded.shape[-1]
    total = None
    for offset in range(27):
        first, second, third = (offset // 9, offset // 3 % 3, offset % 3)
        block = weight[offset * width:(offset + 1) * width]
        rows = window(padded, 2 - first, 2 - second, 2 - third)
        term = lax.dot_general(rows, block, (((1,), (1,)), ((), ())), preferred_element_type=jnp.float32)
        total = term if total is None else total + term
    return total

def weight_terms(padded, grads):
    blocks = []
    for offset in range(27):
        first, second, third = (offset // 9, offset // 3 % 3, offset % 3)
        rows = window(padded, first, second, third)
        blocks.append(lax.dot_general(rows, grads, (((0,), (0,)), ((), ())), preferred_element_type=jnp.float32))
    return jnp.concatenate(blocks, axis=0)

def reference(fields, cotangent, first_weight, second_weight):

    def one_rollout(carry, pair):
        first_acc, second_acc = carry
        field_one, cot_one = pair
        shape = field_one.shape
        width = shape[-1]
        fields_padded = padded_grid(field_one)
        pre = conv_forward(fields_padded, first_weight)
        hidden = gelu_tanh(pre).astype(jnp.bfloat16)
        hidden_padded = padded_grid(hidden.reshape(shape))
        second_out = conv_forward(hidden_padded, second_weight)
        output = (field_one.reshape(-1, width).astype(jnp.float32) + second_out).astype(jnp.bfloat16).reshape(shape)
        cot_flat = cot_one.reshape(-1, width)
        hidden_grad = conv_transposed(padded_grid(cot_one), second_weight)
        second_acc = second_acc + weight_terms(hidden_padded, cot_flat)
        gelu_back = jax.vjp(gelu_tanh, pre)[1]
        pre_grad = gelu_back(hidden_grad)[0].astype(jnp.bfloat16)
        field_term = conv_transposed(padded_grid(pre_grad.reshape(shape)), first_weight)
        field_grad = (cot_flat.astype(jnp.float32) + field_term).astype(jnp.bfloat16).reshape(shape)
        first_acc = first_acc + weight_terms(fields_padded, pre_grad)
        return ((first_acc, second_acc), (output, field_grad))
    zeros = jnp.zeros((KC, C), jnp.float32)
    sums, outs = lax.scan(one_rollout, (zeros, zeros), (fields, cotangent))
    output, field_grad = outs
    return (output, field_grad, sums[0] / ROLL, sums[1] / ROLL)
```

```python
import functools

import jax
import jax.numpy as jnp
from jax import lax
from jax.experimental import pallas as pl
from jax.experimental.pallas import tpu as pltpu
from jax.sharding import PartitionSpec as P

MESH = pl.DeviceIdType.MESH
F32, BF16 = jnp.float32, jnp.bfloat16
DIRS = [(dx, dy) for dx in (-1, 0, 1) for dy in (-1, 0, 1) if dx or dy]
GELU_C = 0.7978845608028654
GELU_A = 0.044715
LAG = 1


def gelu_parts(v):
    return jnp.tanh(GELU_C * (v + GELU_A * (v * v * v)))


def reduction_plan(ndp, kc, steps):
    db = 2 if ndp % 2 == 0 else 1
    da = ndp // db
    rows = kc // ndp
    hops = [(ha, hb) for ha in range(1, da) for hb in range(1, db)]
    hops += [(0, hb) for hb in range(1, db)] + [(ha, 0) for ha in range(1, da)] + [(0, 0)]
    each = kc // steps
    codes, done = [], [0] * ndp
    for d in range(ndp):
        order = []
        for k, (ha, hb) in enumerate(hops):
            p = (d // db + ha) % da * db + (d % db + hb) % db
            for step in range(p * rows // each, -(-(p + 1) * rows // each)):
                if step not in order:
                    order.append(step)
            done[k] = max(done[k], len(order))
        codes.append(sum(step * steps**t for t, step in enumerate(order)))
    first = -(-rows // 256) * 128
    chunks = []
    for side, (low, high) in enumerate(((0, first), (first, rows))):
        middle = low + -(-(high - low) // 256) * 128
        for start, stop in ((low, middle), (middle, high)):
            if stop > start:
                chunks.append((side, start, start - low, stop - start))
    return (da, db), hops, codes, done, chunks


def slot_count(da, db):
    return (db - 1) * da + (da - 1) * db + da - 1 + db - 1


def results(*refs):
    ins, outs, sems = refs[:4], refs[4:8], refs[8]
    copies = [pltpu.make_async_copy(ins[i], outs[i], sems.at[i]) for i in range(4)]
    for copy in copies:
        copy.start()
    for copy in copies:
        copy.wait()


def kernel(
    sizes,
    fields, cot, w1_hbm, w2_hbm,
    out_ref, fgrad_ref, g1_ref, g2_ref,
    w1, w2, p_f, p_c, p_h, p_g, z_a, z_b, z_c, lhs_f, lhs_h, pre,
    own, send_a, recv_a, recv_b, send_z, recv_z,
    sem_w, halo_send, halo_recv, a_send, a_recv, b_send, b_recv, z_send, z_recv,
):
    ndp, npx, npy, rollouts = sizes
    nx, ny, nz, ch = fields.shape
    cells = nx * ny * nz
    half = ch // npy
    kc = own.shape[1]
    rows = kc // ndp
    (da, db), hops, codes, done, chunks = reduction_plan(ndp, kc, 9)
    wid = recv_z.shape[2]
    nj = half // wid
    d, x, y = lax.axis_index("dp"), lax.axis_index("px"), lax.axis_index("py")

    load_w = [
        pltpu.make_async_copy(w1_hbm, w1, sem_w.at[0]),
        pltpu.make_async_copy(w2_hbm, w2, sem_w.at[1]),
    ]
    for copy in load_w:
        copy.start()

    barrier = pltpu.get_barrier_semaphore()
    for i in range(1, ndp):
        pl.semaphore_signal(
            barrier, inc=1, device_id=(lax.rem(d + i, ndp), x, y), device_id_type=MESH
        )
    for i in range(1, npx * npy):
        other = lax.rem(x * npy + y + i, npx * npy)
        pl.semaphore_signal(
            barrier, inc=1, device_id=(d, other // npy, lax.rem(other, npy)), device_id_type=MESH
        )
    pl.semaphore_wait(barrier, ndp - 1 + npx * npy - 1)

    def exists(dx, dy):
        return (x + dx >= 0) & (x + dx < npx) & (y + dy >= 0) & (y + dy < npy)

    def span_src(step, size, base):
        if step == 0:
            return pl.ds(base, size)
        return pl.ds(base if step < 0 else base + size - 1, 1)

    def span_dst(step, size):
        if step == 0:
            return pl.ds(1, size)
        return pl.ds(size + 1 if step < 0 else 0, 1)

    def halo_copy(which, src, base, padded, index):
        dx, dy = DIRS[index]
        return pltpu.make_async_remote_copy(
            src_ref=src.at[span_src(dx, nx, base), span_src(dy, ny, base)],
            dst_ref=padded.at[span_dst(dx, nx), span_dst(dy, ny)],
            send_sem=halo_send.at[which, index],
            recv_sem=halo_recv.at[which, index],
            device_id=(d, x + dx, y + dy),
            device_id_type=MESH,
        )

    def halo_start(which, src, base, padded):
        for index, (dx, dy) in enumerate(DIRS):
            @pl.when(exists(dx, dy))
            def _():
                halo_copy(which, src, base, padded, index).start()

            @pl.when(jnp.logical_not(exists(-dx, -dy)))
            def _():
                sx, sy = span_dst(dx, nx), span_dst(dy, ny)
                padded[sx, sy] = jnp.zeros((sx.size, sy.size, nz, ch), BF16)

    def halo_wait(which, src, base, padded):
        for index, (dx, dy) in enumerate(DIRS):
            @pl.when(exists(dx, dy))
            def _():
                halo_copy(which, src, base, padded, index).wait_send()

            @pl.when(exists(-dx, -dy))
            def _():
                halo_copy(which, src, base, padded, index).wait_recv()

    def build(padded, shifted):
        @pl.loop(0, nx + 2)
        def _(i):
            plane = padded[i]
            flat = plane.reshape((ny + 2) * nz, ch).astype(F32)
            place = lax.broadcasted_iota(jnp.int32, flat.shape, 0) % nz
            low = jnp.where(place == 0, 0.0, pltpu.roll(flat, 1, 0))
            high = jnp.where(place == nz - 1, 0.0, pltpu.roll(flat, flat.shape[0] - 1, 0))
            shifted[i, :, :, 0:ch] = low.astype(BF16).reshape(plane.shape)
            shifted[i, :, :, ch : 2 * ch] = plane
            shifted[i, :, :, 2 * ch : 3 * ch] = high.astype(BF16).reshape(plane.shape)

    tile = ny * nz

    def conv(shifted, weight, flipped, finish, low=0, high=nx):
        @pl.loop(low, high)
        def _(i):
            total = None
            for a in range(3):
                for b in range(3):
                    first = (9 * a + 3 * b) * ch
                    if not flipped:
                        lhs = shifted[i + a, pl.ds(b, ny)].reshape(tile, 3 * ch)
                        term = jnp.dot(
                            lhs, weight[pl.ds(first, 3 * ch)], preferred_element_type=F32
                        )
                        total = term if total is None else total + term
                        continue
                    for c in range(3):
                        lhs = shifted[
                            i + 2 - a, pl.ds(2 - b, ny), :, pl.ds((2 - c) * ch, ch)
                        ].reshape(tile, ch)
                        term = lax.dot_general(
                            lhs,
                            weight[pl.ds(first + c * ch, ch)],
                            (((1,), (1,)), ((), ())),
                            preferred_element_type=F32,
                        )
                        total = term if total is None else total + term
            finish(i, total)

    partner = 1 - y

    def a_copy(which, step):
        part = pl.ds(pl.multiple_of(step * 3 * ch, 3 * ch), 3 * ch)
        return pltpu.make_async_remote_copy(
            src_ref=send_a.at[which, part],
            dst_ref=recv_a.at[which, part],
            send_sem=a_send.at[which, step],
            recv_sem=a_recv.at[which, step],
            device_id=(d, x, partner),
            device_id_type=MESH,
        )

    ia, ib = d // db, lax.rem(d, db)
    code = jnp.int32(codes[0])
    for i in range(1, ndp):
        code = jnp.where(d == i, jnp.int32(codes[i]), code)

    def ring(index, hop, count):
        return lax.rem(index + hop, count) if hop else index

    def piece(ha, hb, chunk):
        first = (ring(ia, ha, da) * db + ring(ib, hb, db)) * rows + chunks[chunk][1]
        return pl.ds(pl.multiple_of(first, 16), chunks[chunk][3])

    def slot_of(phase, side, ha, hb):
        if phase == 0:
            return (hb - 1) * da + ha if side == 0 else (db - 1) * da + (ha - 1) * db + hb
        base = (db - 1) * da + (da - 1) * db
        return base + ha - 1 if side == 0 else base + da - 1 + hb - 1

    def b_copy(which, phase, ha, hb, chunk):
        side, _, offset, size = chunks[chunk]
        if (side == 0) == (phase == 0):
            peer = ia * db + ring(ib, hb, db)
        else:
            peer = ring(ia, ha, da) * db + ib
        slot = slot_of(phase, side, ha, hb)
        return pltpu.make_async_remote_copy(
            src_ref=send_a.at[which, piece(ha, hb, chunk)],
            dst_ref=recv_b.at[which, slot, pl.ds(offset, size)],
            send_sem=b_send.at[which, slot, chunk],
            recv_sem=b_recv.at[which, slot, chunk],
            device_id=(peer, x, y),
            device_id_type=MESH,
        )

    def arrived(which, phase, ha, hb, chunk):
        side, _, offset, size = chunks[chunk]
        b_copy(which, phase, ha, hb, chunk).wait_recv()
        return recv_b[which, slot_of(phase, side, ha, hb), pl.ds(offset, size)].astype(F32)

    def piece_start(which, k):
        for t in range(done[k - 1] if k else 0, done[k]):
            a_copy(which, lax.rem(code // 9**t, 9)).wait()
        ha, hb = hops[k]
        for chunk, (side, _, _, _) in enumerate(chunks):
            part = piece(ha, hb, chunk)
            total = own[which, part] + recv_a[which, part].astype(F32)
            if (hb if side == 0 else ha) > 0:
                send_a[which, part] = total.astype(BF16)
                b_copy(which, 0, ha, hb, chunk).start()
            else:
                own[which, part] = total

    def weight_grad(which, lhs, shifted):
        def one(t, left):
            for k in range(len(hops)):
                if done[k] + LAG < 9:
                    @pl.when(t == done[k] + LAG)
                    def _():
                        piece_start(which, k)
            step = lax.rem(left, 9)
            a, b = step // 3, lax.rem(step, 3)
            rhs = shifted[pl.ds(2 - a, nx), pl.ds(2 - b, ny)].reshape(cells, 3 * ch)
            prod = jnp.dot(lhs[...], rhs, preferred_element_type=F32)
            for c in range(3):
                block = prod[:, (2 - c) * ch : (3 - c) * ch]
                here = pl.ds(pl.multiple_of(step * 3 * ch, ch) + c * ch, ch)
                low, high = block[:, :half], block[:, half:]
                own[which, here] = jnp.where(y == 0, low, high)
                send_a[which, here] = jnp.where(y == 0, high, low).astype(BF16)
            a_copy(which, step).start()
            return left // 9

        lax.fori_loop(0, 9, one, code)

    def pieces_rest(which):
        for k in range(len(hops)):
            if done[k] + LAG >= 9:
                piece_start(which, k)

    def relay(which, chunk):
        side = chunks[chunk][0]
        for hop in range(1, da if side == 0 else db):
            ha, hb = (hop, 0) if side == 0 else (0, hop)
            part = piece(ha, hb, chunk)
            total = own[which, part]
            for first in range(1, db if side == 0 else da):
                fa, fb = (hop, first) if side == 0 else (first, hop)
                total = total + arrived(which, 0, fa, fb, chunk)
            send_a[which, part] = total.astype(BF16)
            b_copy(which, 1, ha, hb, chunk).start()

    def z_ids(j):
        owner = y * nj + j
        return owner // npy, lax.rem(owner, npy)

    def lanes(chunk):
        return pl.ds(chunks[chunk][1], -(-chunks[chunk][3] // 128) * 128)

    def z_remote(which, j, chunk):
        px_o, py_o = z_ids(j)
        return pltpu.make_async_remote_copy(
            src_ref=send_z.at[which, pl.ds(j * wid, wid), lanes(chunk)],
            dst_ref=recv_z.at[which, x, :, lanes(chunk)],
            send_sem=z_send.at[which, j, chunk],
            recv_sem=z_recv.at[which, x, chunk],
            device_id=(d, px_o, py_o),
            device_id_type=MESH,
        )

    def columns_start(which, chunk):
        side, _, _, size = chunks[chunk]
        total = own[which, piece(0, 0, chunk)]
        for hop in range(1, db if side == 0 else da):
            total = total + arrived(which, 0, *((0, hop) if side == 0 else (hop, 0)), chunk)
        for hop in range(1, da if side == 0 else db):
            total = total + arrived(which, 1, *((hop, 0) if side == 0 else (0, hop)), chunk)
        pad = -size % 128
        if pad:
            total = jnp.concatenate([total, jnp.zeros((pad, half), F32)], axis=0)
        send_z[which, :, lanes(chunk)] = total.T.astype(BF16)
        for j in range(nj):
            px_o, py_o = z_ids(j)
            mine = (px_o == x) & (py_o == y)

            @pl.when(jnp.logical_not(mine))
            def _():
                z_remote(which, j, chunk).start()

            @pl.when(mine)
            def _():
                pltpu.make_async_copy(
                    send_z.at[which, pl.ds(j * wid, wid), lanes(chunk)],
                    recv_z.at[which, x, :, lanes(chunk)],
                    z_recv.at[which, x, chunk],
                ).start()

    def finish_grad(which, grad, chunk):
        total = None
        for i in range(npx):
            here = recv_z.at[which, i, :, lanes(chunk)]
            pltpu.make_async_copy(here, here, z_recv.at[which, i, chunk]).wait()
            term = recv_z[which, i, :, lanes(chunk)].astype(F32)
            total = term if total is None else total + term
        _, start, _, size = chunks[chunk]
        grad[:, start : start + size] = (total / rollouts)[:, :size]

    def sent(which):
        for chunk, (side, _, _, _) in enumerate(chunks):
            for ha, hb in hops:
                if (hb if side == 0 else ha) > 0:
                    b_copy(which, 0, ha, hb, chunk).wait_send()
            for hop in range(1, da if side == 0 else db):
                b_copy(which, 1, *((hop, 0) if side == 0 else (0, hop)), chunk).wait_send()
            for j in range(nj):
                px_o, py_o = z_ids(j)

                @pl.when(jnp.logical_not((px_o == x) & (py_o == y)))
                def _():
                    z_remote(which, j, chunk).wait_send()

    every = range(len(chunks))

    halo_start(0, fields, 0, p_f)
    halo_start(1, cot, 0, p_c)
    p_f[pl.ds(1, nx), pl.ds(1, ny)] = fields[...]
    p_c[pl.ds(1, nx), pl.ds(1, ny)] = cot[...]
    lhs_f[...] = fields[...].reshape(cells, ch).T
    halo_wait(0, fields, 0, p_f)
    build(p_f, z_a)
    load_w[0].wait()

    def hidden_finish(i, total):
        pre[i] = total
        value = (total * (0.5 * (1.0 + gelu_parts(total)))).astype(BF16)
        p_h[i + 1, pl.ds(1, ny)] = value.reshape(ny, nz, ch)

    conv(z_a, w1, False, hidden_finish)
    halo_start(2, p_h, 1, p_h)
    lhs_h[...] = p_h[pl.ds(1, nx), pl.ds(1, ny)].reshape(cells, ch).T
    halo_wait(1, cot, 0, p_c)
    build(p_c, z_b)
    weight_grad(1, lhs_h, z_b)
    pieces_rest(1)
    load_w[1].wait()

    def grad_finish(i, total):
        v = pre[i]
        t = gelu_parts(v)
        slope = 0.5 * (1.0 + t) + (0.5 * v) * (1.0 - t * t) * (
            GELU_C * (1.0 + (3.0 * GELU_A) * (v * v))
        )
        p_g[i + 1, pl.ds(1, ny)] = (total * slope).astype(BF16).reshape(ny, nz, ch)

    conv(z_b, w2, True, grad_finish)
    halo_start(3, p_g, 1, p_g)
    for chunk in every:
        relay(1, chunk)
    halo_wait(2, p_h, 1, p_h)
    build(p_h, z_a)

    def out_finish(i, total):
        out_ref[i] = (
            (fields[i].reshape(tile, ch).astype(F32) + total).astype(BF16).reshape(ny, nz, ch)
        )

    conv(z_a, w2, False, out_finish, 0, nx // 2)
    halo_wait(3, p_g, 1, p_g)
    build(p_g, z_c)
    weight_grad(0, lhs_f, z_c)
    pieces_rest(0)
    for chunk in every:
        columns_start(1, chunk)
    conv(z_a, w2, False, out_finish, nx // 2, nx)

    def field_finish(i, total):
        fgrad_ref[i] = (
            (cot[i].reshape(tile, ch).astype(F32) + total).astype(BF16).reshape(ny, nz, ch)
        )

    conv(z_c, w1, True, field_finish, 0, nx // 2)
    for chunk in every:
        relay(0, chunk)
    conv(z_c, w1, True, field_finish, nx // 2, nx)
    for chunk in every:
        finish_grad(1, g2_ref, chunk)
    sent(1)
    for chunk in every:
        columns_start(0, chunk)
    for chunk in every:
        finish_grad(0, g1_ref, chunk)
    sent(0)


def body(sizes, fields, cotangent, first_weight, second_weight):
    ndp, npx, npy = sizes
    batch, nx, ny, nz, ch = fields.shape
    kc = first_weight.shape[0]
    half = ch // npy
    (da, db), _, _, _, chunks = reduction_plan(ndp, kc, 9)
    slots = slot_count(da, db)
    longest = max(offset + size for _, _, offset, size in chunks)
    rows = kc // ndp
    rpad = -(-rows // 128) * 128
    wid = ch // (npx * npy)
    cells = nx * ny * nz
    vmem = pl.BlockSpec(memory_space=pltpu.VMEM)
    hbm = pl.BlockSpec(memory_space=pl.ANY)
    padded = pltpu.VMEM((nx + 2, ny + 2, nz, ch), BF16)
    shifted = pltpu.VMEM((nx + 2, ny + 2, nz, 3 * ch), BF16)
    dma = pltpu.SemaphoreType.DMA
    block = (nx, ny, nz, ch)
    out, fgrad, g1, g2 = pl.pallas_call(
        functools.partial(kernel, (ndp, npx, npy, batch * ndp)),
        out_shape=(
            jax.ShapeDtypeStruct(block, BF16),
            jax.ShapeDtypeStruct(block, BF16),
            jax.ShapeDtypeStruct((wid, rows), F32),
            jax.ShapeDtypeStruct((wid, rows), F32),
        ),
        in_specs=[vmem, vmem, hbm, hbm],
        out_specs=(vmem, vmem, vmem, vmem),
        scratch_shapes=[
            pltpu.VMEM((kc, ch), BF16),
            pltpu.VMEM((kc, ch), BF16),
            padded, padded, padded, padded,
            shifted, shifted, shifted,
            pltpu.VMEM((ch, cells), BF16),
            pltpu.VMEM((ch, cells), BF16),
            pltpu.VMEM((nx, ny * nz, ch), F32),
            pltpu.VMEM((2, kc, half), F32),
            pltpu.VMEM((2, kc, half), BF16),
            pltpu.VMEM((2, kc, half), BF16),
            pltpu.VMEM((2, slots, longest, half), BF16),
            pltpu.VMEM((2, half, rpad), BF16),
            pltpu.VMEM((2, npx, wid, rpad), BF16),
            dma((2,)),
            dma((4, 8)), dma((4, 8)),
            dma((2, 9)), dma((2, 9)),
            dma((2, slots, len(chunks))), dma((2, slots, len(chunks))),
            dma((2, half // wid, len(chunks))), dma((2, npx, len(chunks))),
        ],
        compiler_params=pltpu.CompilerParams(
            collective_id=0, has_side_effects=True, vmem_limit_bytes=64000000
        ),
        name="closure",
    )(fields.reshape(block), cotangent.reshape(block), first_weight, second_weight)
    out, fgrad, g1, g2 = pl.pallas_call(
        results,
        out_shape=(
            jax.ShapeDtypeStruct(block, BF16),
            jax.ShapeDtypeStruct(block, BF16),
            jax.ShapeDtypeStruct((wid, rows), F32),
            jax.ShapeDtypeStruct((wid, rows), F32),
        ),
        in_specs=[hbm] * 4,
        out_specs=(hbm,) * 4,
        scratch_shapes=[dma((4,))],
        name="results",
    )(out, fgrad, g1, g2)
    return (
        out.reshape(fields.shape),
        fgrad.reshape(fields.shape),
        g1.T,
        g2.T,
    )


def solution(mesh):
    sizes = tuple(mesh.shape[name] for name in ("dp", "px", "py"))
    placed = (P("dp", "px", "py", None, None), P("dp", "px", "py", None, None), P(), P())
    return jax.shard_map(
        functools.partial(body, sizes),
        mesh=mesh,
        in_specs=placed,
        out_specs=(
            P("dp", "px", "py", None, None),
            P("dp", "px", "py", None, None),
            P("dp", ("px", "py")),
            P("dp", ("px", "py")),
        ),
        check_vma=False,
    )
```

```python
import functools

import jax
import jax.numpy as jnp
from jax import lax
from jax.experimental import pallas as pl
from jax.experimental.pallas import tpu as pltpu
from jax.sharding import PartitionSpec as P

MESH = pl.DeviceIdType.MESH
F32, BF16 = jnp.float32, jnp.bfloat16
DIRS = [(dx, dy) for dx in (-1, 0, 1) for dy in (-1, 0, 1) if dx or dy]
ALONG = [i for i, (dx, _) in enumerate(DIRS) if dx]
ACROSS = [i for i, (dx, _) in enumerate(DIRS) if not dx]
GELU_C = 0.7978845608028654
GELU_A = 0.044715
LAG = 2


def gelu_parts(v):
    return jnp.tanh(GELU_C * (v + GELU_A * (v * v * v)))


def reduction_plan(ndp, kc, steps):
    db = 2 if ndp % 2 == 0 else 1
    da = ndp // db
    rows = kc // ndp
    hops = [(ha, hb) for ha in range(1, da) for hb in range(1, db)]
    hops += [(0, hb) for hb in range(1, db)] + [(ha, 0) for ha in range(1, da)] + [(0, 0)]
    each = kc // steps
    codes, done = [], [0] * ndp
    for d in range(ndp):
        order = []
        for k, (ha, hb) in enumerate(hops):
            p = (d // db + ha) % da * db + (d % db + hb) % db
            for step in range(p * rows // each, -(-(p + 1) * rows // each)):
                if step not in order:
                    order.append(step)
            done[k] = max(done[k], len(order))
        codes.append(sum(step * steps**t for t, step in enumerate(order)))
    first = -(-rows // 256) * 128
    chunks = []
    for side, (low, high) in enumerate(((0, first), (first, rows))):
        tiles, start = -(-(high - low) // 128), low
        for left in range(min(3, tiles), 0, -1):
            stop = min(high, start + -(-tiles // left) * 128)
            tiles -= -(-tiles // left)
            chunks.append((side, start, start - low, stop - start))
            start = stop
    return (da, db), hops, codes, done, chunks


def slot_count(da, db):
    return (db - 1) * da + (da - 1) * db + da - 1 + db - 1


def results(*refs):
    ins, outs, sems = refs[:4], refs[4:8], refs[8]
    copies = [pltpu.make_async_copy(ins[i], outs[i], sems.at[i]) for i in range(4)]
    for copy in copies:
        copy.start()
    for copy in copies:
        copy.wait()


def kernel(
    sizes,
    fields, cot, w1_hbm, w2_hbm,
    out_ref, fgrad_ref, g1_ref, g2_ref,
    w1, w2, p_f, p_c, p_h, p_g, z_a, z_b, z_c, lhs_f, lhs_h, pre,
    own, send_a, recv_a, recv_b, send_z, recv_z,
    sem_w, halo_send, halo_recv, a_send, a_recv, b_send, b_recv, z_send, z_recv,
):
    ndp, npx, npy, rollouts = sizes
    nx, ny, nz, ch = fields.shape
    cells = nx * ny * nz
    half = ch // npy
    kc = own.shape[1]
    rows = kc // ndp
    (da, db), hops, codes, done, chunks = reduction_plan(ndp, kc, 9)
    wid = recv_z[0].shape[2]
    nj = half // wid
    d, x, y = lax.axis_index("dp"), lax.axis_index("px"), lax.axis_index("py")

    inner = pl.ds(1, nx), pl.ds(1, ny)
    load_f = pltpu.make_async_copy(fields, p_f.at[inner], sem_w.at[2])
    load_c = pltpu.make_async_copy(cot, p_c.at[inner], sem_w.at[3])
    load_w = [
        pltpu.make_async_copy(w1_hbm, w1, sem_w.at[0]),
        pltpu.make_async_copy(w2_hbm, w2, sem_w.at[1]),
    ]
    for copy in [load_f, load_c, *load_w]:
        copy.start()

    barrier = pltpu.get_barrier_semaphore()
    for i in range(1, ndp):
        pl.semaphore_signal(
            barrier, inc=1, device_id=(lax.rem(d + i, ndp), x, y), device_id_type=MESH
        )
    for i in range(1, npx * npy):
        other = lax.rem(x * npy + y + i, npx * npy)
        pl.semaphore_signal(
            barrier, inc=1, device_id=(d, other // npy, lax.rem(other, npy)), device_id_type=MESH
        )
    pl.semaphore_wait(barrier, ndp - 1 + npx * npy - 1)

    def exists(dx, dy):
        return (x + dx >= 0) & (x + dx < npx) & (y + dy >= 0) & (y + dy < npy)

    def span_src(step, size, base):
        if step == 0:
            return pl.ds(base, size)
        return pl.ds(base if step < 0 else base + size - 1, 1)

    def span_dst(step, size):
        if step == 0:
            return pl.ds(1, size)
        return pl.ds(size + 1 if step < 0 else 0, 1)

    def halo_copy(which, src, base, padded, index):
        dx, dy = DIRS[index]
        return pltpu.make_async_remote_copy(
            src_ref=src.at[span_src(dx, nx, base), span_src(dy, ny, base)],
            dst_ref=padded.at[span_dst(dx, nx), span_dst(dy, ny)],
            send_sem=halo_send.at[which, index],
            recv_sem=halo_recv.at[which, index],
            device_id=(d, x + dx, y + dy),
            device_id_type=MESH,
        )

    def halo_start(which, src, base, padded, group):
        for index in group:
            dx, dy = DIRS[index]

            @pl.when(exists(dx, dy))
            def _():
                halo_copy(which, src, base, padded, index).start()

            @pl.when(jnp.logical_not(exists(-dx, -dy)))
            def _():
                sx, sy = span_dst(dx, nx), span_dst(dy, ny)
                padded[sx, sy] = jnp.zeros((sx.size, sy.size, nz, ch), BF16)

    def halo_wait(which, src, base, padded, group):
        for index in group:
            dx, dy = DIRS[index]

            @pl.when(exists(dx, dy))
            def _():
                halo_copy(which, src, base, padded, index).wait_send()

            @pl.when(exists(-dx, -dy))
            def _():
                halo_copy(which, src, base, padded, index).wait_recv()

    def build(padded, shifted, low, high, stride=1):
        @pl.loop(low, high)
        def _(j):
            i = j * stride
            plane = padded[i]
            flat = plane.reshape((ny + 2) * nz, ch).astype(F32)
            place = lax.broadcasted_iota(jnp.int32, flat.shape, 0) % nz
            before = jnp.where(place == 0, 0.0, pltpu.roll(flat, 1, 0))
            after = jnp.where(place == nz - 1, 0.0, pltpu.roll(flat, flat.shape[0] - 1, 0))
            shifted[i, :, :, 0:ch] = before.astype(BF16).reshape(plane.shape)
            shifted[i, :, :, ch : 2 * ch] = plane
            shifted[i, :, :, 2 * ch : 3 * ch] = after.astype(BF16).reshape(plane.shape)

    tile = ny * nz

    def conv(shifted, weight, flipped, finish, *planes):
        step = planes[1] - planes[0] if len(planes) > 1 else 1

        @pl.loop(0, len(planes))
        def _(j):
            i = planes[0] + j * step
            total = None
            for a in range(3):
                for b in range(3):
                    first = (9 * a + 3 * b) * ch
                    if not flipped:
                        lhs = shifted[i + a, pl.ds(b, ny)].reshape(tile, 3 * ch)
                        term = jnp.dot(
                            lhs, weight[pl.ds(first, 3 * ch)], preferred_element_type=F32
                        )
                        total = term if total is None else total + term
                        continue
                    for c in range(3):
                        lhs = shifted[
                            i + 2 - a, pl.ds(2 - b, ny), :, pl.ds((2 - c) * ch, ch)
                        ].reshape(tile, ch)
                        term = lax.dot_general(
                            lhs,
                            weight[pl.ds(first + c * ch, ch)],
                            (((1,), (1,)), ((), ())),
                            preferred_element_type=F32,
                        )
                        total = term if total is None else total + term
            finish(i, total)

    edges, middle = sorted({0, nx - 1}), range(1, nx - 1)
    partner = 1 - y

    def a_copy(which, step):
        part = pl.ds(pl.multiple_of(step * 3 * ch, 3 * ch), 3 * ch)
        return pltpu.make_async_remote_copy(
            src_ref=send_a.at[which, part],
            dst_ref=recv_a.at[which, part],
            send_sem=a_send.at[which, step],
            recv_sem=a_recv.at[which, step],
            device_id=(d, x, partner),
            device_id_type=MESH,
        )

    ia, ib = d // db, lax.rem(d, db)
    groups = [[], [], []]
    for side in range(2):
        here = [chunk for chunk in range(len(chunks)) if chunks[chunk][0] == side]
        for order, chunk in enumerate(here):
            groups[order].append(chunk)
    code = jnp.int32(codes[0])
    for i in range(1, ndp):
        code = jnp.where(d == i, jnp.int32(codes[i]), code)

    def ring(index, hop, count):
        return lax.rem(index + hop, count) if hop else index

    def piece(ha, hb, chunk):
        first = (ring(ia, ha, da) * db + ring(ib, hb, db)) * rows + chunks[chunk][1]
        return pl.ds(pl.multiple_of(first, 16), chunks[chunk][3])

    def slot_of(phase, side, ha, hb):
        if phase == 0:
            return (hb - 1) * da + ha if side == 0 else (db - 1) * da + (ha - 1) * db + hb
        base = (db - 1) * da + (da - 1) * db
        return base + ha - 1 if side == 0 else base + da - 1 + hb - 1

    def b_copy(which, phase, ha, hb, chunk):
        side, _, offset, size = chunks[chunk]
        if (side == 0) == (phase == 0):
            peer = ia * db + ring(ib, hb, db)
        else:
            peer = ring(ia, ha, da) * db + ib
        slot = slot_of(phase, side, ha, hb)
        return pltpu.make_async_remote_copy(
            src_ref=send_a.at[which, piece(ha, hb, chunk)],
            dst_ref=recv_b.at[which, slot, pl.ds(offset, size)],
            send_sem=b_send.at[which, slot, chunk],
            recv_sem=b_recv.at[which, slot, chunk],
            device_id=(peer, x, y),
            device_id_type=MESH,
        )

    def arrived(which, phase, ha, hb, chunk):
        side, _, offset, size = chunks[chunk]
        b_copy(which, phase, ha, hb, chunk).wait_recv()
        return recv_b[which, slot_of(phase, side, ha, hb), pl.ds(offset, size)].astype(F32)

    def piece_start(which, k):
        for t in range(done[k - 1] if k else 0, done[k]):
            a_copy(which, lax.rem(code // 9**t, 9)).wait()
        ha, hb = hops[k]
        for chunk, (side, _, _, _) in enumerate(chunks):
            part = piece(ha, hb, chunk)
            total = own[which, part] + recv_a[which, part].astype(F32)
            if (hb if side == 0 else ha) > 0:
                send_a[which, part] = total.astype(BF16)
                if chunk in groups[0] or (ha and hb and chunk in groups[1]):
                    b_copy(which, 0, ha, hb, chunk).start()
            else:
                own[which, part] = total

    def pieces_send(which, diagonal, order):
        for ha, hb in hops:
            if order < len(groups) and (ha > 0 and hb > 0) == diagonal:
                for chunk in groups[order]:
                    if (hb if chunks[chunk][0] == 0 else ha) > 0:
                        b_copy(which, 0, ha, hb, chunk).start()

    def weight_grad(which, lhs, shifted, beside):
        def one(t, left):
            for at, task in beside:
                @pl.when(t == at)
                def _():
                    task()

            for k in range(len(hops)):
                if done[k] + LAG < 9:
                    @pl.when(t == done[k] + LAG)
                    def _():
                        piece_start(which, k)
            step = lax.rem(left, 9)
            a, b = step // 3, lax.rem(step, 3)
            rhs = shifted[pl.ds(2 - a, nx), pl.ds(2 - b, ny)].reshape(cells, 3 * ch)
            prod = jnp.dot(lhs[...], rhs, preferred_element_type=F32)
            for c in range(3):
                block = prod[:, (2 - c) * ch : (3 - c) * ch]
                here = pl.ds(pl.multiple_of(step * 3 * ch, ch) + c * ch, ch)
                low, high = block[:, :half], block[:, half:]
                own[which, here] = jnp.where(y == 0, low, high)
                send_a[which, here] = jnp.where(y == 0, high, low).astype(BF16)
            a_copy(which, step).start()
            return left // 9

        lax.fori_loop(0, 9, one, code)

    def pieces_rest(which):
        for k in range(len(hops)):
            if done[k] + LAG >= 9 and k < len(hops) - 1:
                piece_start(which, k)

    def own_piece(which):
        piece_start(which, len(hops) - 1)

    def advance(which, order):
        for chunk in groups[order]:
            relay(which, chunk)
        pieces_send(which, True, order + 2)
        pieces_send(which, False, order + 1)

    def relay(which, chunk):
        side = chunks[chunk][0]
        for hop in range(1, da if side == 0 else db):
            ha, hb = (hop, 0) if side == 0 else (0, hop)
            part = piece(ha, hb, chunk)
            total = own[which, part]
            for first in range(1, db if side == 0 else da):
                fa, fb = (hop, first) if side == 0 else (first, hop)
                total = total + arrived(which, 0, fa, fb, chunk)
            send_a[which, part] = total.astype(BF16)
            b_copy(which, 1, ha, hb, chunk).start()

    def z_ids(j):
        owner = y * nj + j
        return owner // npy, lax.rem(owner, npy)

    def z_remote(which, j, chunk):
        px_o, py_o = z_ids(j)
        return pltpu.make_async_remote_copy(
            src_ref=send_z[chunk].at[which, pl.ds(j * wid, wid)],
            dst_ref=recv_z[chunk].at[which, x],
            send_sem=z_send.at[which, j, chunk],
            recv_sem=z_recv.at[which, x, chunk],
            device_id=(d, px_o, py_o),
            device_id_type=MESH,
        )

    def columns_start(which, chunk):
        side, _, _, size = chunks[chunk]
        total = own[which, piece(0, 0, chunk)]
        for hop in range(1, db if side == 0 else da):
            total = total + arrived(which, 0, *((0, hop) if side == 0 else (hop, 0)), chunk)
        for hop in range(1, da if side == 0 else db):
            total = total + arrived(which, 1, *((hop, 0) if side == 0 else (0, hop)), chunk)
        pad = -size % 128
        if pad:
            total = jnp.concatenate([total, jnp.zeros((pad, half), F32)], axis=0)
        send_z[chunk][which] = total.T.astype(BF16)
        for j in range(nj):
            px_o, py_o = z_ids(j)
            mine = (px_o == x) & (py_o == y)

            @pl.when(jnp.logical_not(mine))
            def _():
                z_remote(which, j, chunk).start()

            @pl.when(mine)
            def _():
                recv_z[chunk][which, x] = send_z[chunk][which, j * wid : (j + 1) * wid]

    def columns_send(which, order):
        for chunk in groups[order]:
            columns_start(which, chunk)

    def finish_grad(which, grad, chunk):
        total = None
        for i in range(npx):
            here = recv_z[chunk].at[which, i]

            @pl.when((x != i) | (y != (x * npy + y) // nj))
            def _():
                pltpu.make_async_copy(here, here, z_recv.at[which, i, chunk]).wait()

            term = recv_z[chunk][which, i].astype(F32)
            total = term if total is None else total + term
        _, start, _, size = chunks[chunk]
        grad[:, start : start + size] = (total / rollouts)[:, :size]

    def sent(which):
        for chunk, (side, _, _, _) in enumerate(chunks):
            for ha, hb in hops:
                if (hb if side == 0 else ha) > 0:
                    b_copy(which, 0, ha, hb, chunk).wait_send()
            for hop in range(1, da if side == 0 else db):
                b_copy(which, 1, *((hop, 0) if side == 0 else (0, hop)), chunk).wait_send()
            for j in range(nj):
                px_o, py_o = z_ids(j)

                @pl.when(jnp.logical_not((px_o == x) & (py_o == y)))
                def _():
                    z_remote(which, j, chunk).wait_send()

    every = range(len(chunks))

    load_f.wait()
    halo_start(0, p_f, 1, p_f, ALONG)
    halo_start(0, p_f, 1, p_f, ACROSS)
    load_c.wait()
    halo_start(1, p_c, 1, p_c, ACROSS)
    halo_wait(0, p_f, 1, p_f, ACROSS)
    build(p_f, z_a, 1, nx + 1)

    def hidden_finish(i, total):
        pre[i] = total
        value = (total * (0.5 * (1.0 + gelu_parts(total)))).astype(BF16)
        p_h[i + 1, pl.ds(1, ny)] = value.reshape(ny, nz, ch)

    load_w[0].wait()
    conv(z_a, w1, False, hidden_finish, *middle)
    halo_start(1, p_c, 1, p_c, ALONG)
    halo_wait(1, p_c, 1, p_c, ACROSS)
    build(p_c, z_b, 1, nx + 1)
    halo_wait(0, p_f, 1, p_f, ALONG)
    build(p_f, z_a, 0, 2, nx + 1)
    conv(z_a, w1, False, hidden_finish, *edges)
    halo_start(2, p_h, 1, p_h, ALONG)
    halo_start(2, p_h, 1, p_h, ACROSS)
    lhs_h[...] = p_h[pl.ds(1, nx), pl.ds(1, ny)].reshape(cells, ch).T
    halo_wait(1, p_c, 1, p_c, ALONG)
    build(p_c, z_b, 0, 2, nx + 1)
    weight_grad(1, lhs_h, z_b, [])
    pieces_rest(1)
    advance(1, 0)
    load_w[1].wait()

    def grad_finish(i, total):
        v = pre[i]
        t = gelu_parts(v)
        slope = 0.5 * (1.0 + t) + (0.5 * v) * (1.0 - t * t) * (
            GELU_C * (1.0 + (3.0 * GELU_A) * (v * v))
        )
        p_g[i + 1, pl.ds(1, ny)] = (total * slope).astype(BF16).reshape(ny, nz, ch)

    conv(z_b, w2, True, grad_finish, *edges)
    halo_start(3, p_g, 1, p_g, ALONG)
    own_piece(1)
    advance(1, 1)
    conv(z_b, w2, True, grad_finish, *middle)
    halo_start(3, p_g, 1, p_g, ACROSS)
    lhs_f[...] = p_f[inner].reshape(cells, ch).T
    halo_wait(2, p_h, 1, p_h, ALONG)
    halo_wait(2, p_h, 1, p_h, ACROSS)
    build(p_h, z_a, 0, nx + 2)
    columns_send(1, 0)

    def out_finish(i, total):
        out_ref[i] = (
            (p_f[i + 1, pl.ds(1, ny)].reshape(tile, ch).astype(F32) + total).astype(BF16).reshape(ny, nz, ch)
        )

    conv(z_a, w2, False, out_finish, *range(nx // 2))
    advance(1, 2)
    halo_wait(3, p_g, 1, p_g, ACROSS)
    build(p_g, z_c, 1, nx + 1)
    halo_wait(3, p_g, 1, p_g, ALONG)
    build(p_g, z_c, 0, 2, nx + 1)
    weight_grad(
        0, lhs_f, z_c,
        [(1, lambda: columns_send(1, 1)), (7, lambda: columns_send(1, 2))],
    )
    pieces_rest(0)
    advance(0, 0)
    conv(z_a, w2, False, out_finish, *range(nx // 2, nx))
    own_piece(0)
    advance(0, 1)

    def field_finish(i, total):
        fgrad_ref[i] = (
            (p_c[i + 1, pl.ds(1, ny)].reshape(tile, ch).astype(F32) + total).astype(BF16).reshape(ny, nz, ch)
        )

    conv(z_c, w1, True, field_finish, *edges)
    columns_send(0, 0)
    advance(0, 2)
    conv(z_c, w1, True, field_finish, *middle)
    for chunk in every:
        finish_grad(1, g2_ref, chunk)
    sent(1)
    columns_send(0, 1)
    columns_send(0, 2)
    for chunk in groups[0] + groups[1] + groups[2]:
        finish_grad(0, g1_ref, chunk)
    sent(0)


def body(sizes, fields, cotangent, first_weight, second_weight):
    ndp, npx, npy = sizes
    batch, nx, ny, nz, ch = fields.shape
    kc = first_weight.shape[0]
    half = ch // npy
    (da, db), _, _, _, chunks = reduction_plan(ndp, kc, 9)
    slots = slot_count(da, db)
    longest = max(offset + size for _, _, offset, size in chunks)
    rows = kc // ndp
    widths = [-(-size // 128) * 128 for _, _, _, size in chunks]
    wid = ch // (npx * npy)
    cells = nx * ny * nz
    vmem = pl.BlockSpec(memory_space=pltpu.VMEM)
    hbm = pl.BlockSpec(memory_space=pltpu.HBM)
    anywhere = pl.BlockSpec(memory_space=pl.ANY)
    padded = pltpu.VMEM((nx + 2, ny + 2, nz, ch), BF16)
    shifted = pltpu.VMEM((nx + 2, ny + 2, nz, 3 * ch), BF16)
    dma = pltpu.SemaphoreType.DMA
    block = (nx, ny, nz, ch)
    out, fgrad, g1, g2 = pl.pallas_call(
        functools.partial(kernel, (ndp, npx, npy, batch * ndp)),
        out_shape=(
            jax.ShapeDtypeStruct(block, BF16),
            jax.ShapeDtypeStruct(block, BF16),
            jax.ShapeDtypeStruct((wid, rows), F32),
            jax.ShapeDtypeStruct((wid, rows), F32),
        ),
        in_specs=[hbm] * 4,
        out_specs=(vmem, vmem, vmem, vmem),
        scratch_shapes=[
            pltpu.VMEM((kc, ch), BF16),
            pltpu.VMEM((kc, ch), BF16),
            padded, padded, padded, padded,
            shifted, shifted, shifted,
            pltpu.VMEM((ch, cells), BF16),
            pltpu.VMEM((ch, cells), BF16),
            pltpu.VMEM((nx, ny * nz, ch), F32),
            pltpu.VMEM((2, kc, half), F32),
            pltpu.VMEM((2, kc, half), BF16),
            pltpu.VMEM((2, kc, half), BF16),
            pltpu.VMEM((2, slots, longest, half), BF16),
            [pltpu.VMEM((2, half, width), BF16) for width in widths],
            [pltpu.VMEM((2, npx, wid, width), BF16) for width in widths],
            dma((4,)),
            dma((4, 8)), dma((4, 8)),
            dma((2, 9)), dma((2, 9)),
            dma((2, slots, len(chunks))), dma((2, slots, len(chunks))),
            dma((2, half // wid, len(chunks))), dma((2, npx, len(chunks))),
        ],
        compiler_params=pltpu.CompilerParams(
            collective_id=0, has_side_effects=True, vmem_limit_bytes=48000000
        ),
        name="closure",
    )(*(pltpu.with_memory_space_constraint(v, pltpu.HBM) for v in (fields.reshape(block), cotangent.reshape(block), first_weight, second_weight)))
    out, fgrad, g1, g2 = pl.pallas_call(
        results,
        out_shape=(
            jax.ShapeDtypeStruct(block, BF16),
            jax.ShapeDtypeStruct(block, BF16),
            jax.ShapeDtypeStruct((wid, rows), F32),
            jax.ShapeDtypeStruct((wid, rows), F32),
        ),
        in_specs=[anywhere] * 4,
        out_specs=(hbm,) * 4,
        scratch_shapes=[dma((4,))],
        compiler_params=pltpu.CompilerParams(vmem_limit_bytes=1 << 20),
        name="results",
    )(out, fgrad, g1, g2)
    return (
        out.reshape(fields.shape),
        fgrad.reshape(fields.shape),
        g1.T,
        g2.T,
    )


def solution(mesh):
    sizes = tuple(mesh.shape[name] for name in ("dp", "px", "py"))
    placed = (P("dp", "px", "py", None, None), P("dp", "px", "py", None, None), P(), P())
    return jax.shard_map(
        functools.partial(body, sizes),
        mesh=mesh,
        in_specs=placed,
        out_specs=(
            P("dp", "px", "py", None, None),
            P("dp", "px", "py", None, None),
            P("dp", ("px", "py")),
            P("dp", ("px", "py")),
        ),
        check_vma=False,
    )
```

```python
import functools

import jax
import jax.numpy as jnp
from jax import lax
from jax.experimental import pallas as pl
from jax.experimental.pallas import tpu as pltpu
from jax.sharding import PartitionSpec as P

MESH = pl.DeviceIdType.MESH
F32, BF16 = jnp.float32, jnp.bfloat16
DIRS = [(dx, dy) for dx in (-1, 0, 1) for dy in (-1, 0, 1) if dx or dy]
ALONG = [i for i, (dx, _) in enumerate(DIRS) if dx]
ACROSS = [i for i, (dx, _) in enumerate(DIRS) if not dx]
GELU_C = 0.7978845608028654
GELU_A = 0.044715
LAG = 1
LOADS = 4


def gelu_parts(v):
    return jnp.tanh(GELU_C * (v + GELU_A * (v * v * v)))


def reduction_plan(ndp, kc, steps):
    db = 2 if ndp % 2 == 0 else 1
    da = ndp // db
    rows = kc // ndp
    hops = [(ha, hb) for ha in range(1, da) for hb in range(1, db)]
    hops += [(0, hb) for hb in range(1, db)] + [(ha, 0) for ha in range(1, da)] + [(0, 0)]
    each = kc // steps
    codes, done = [], [0] * ndp
    for d in range(ndp):
        order = []
        for k, (ha, hb) in enumerate(hops):
            p = (d // db + ha) % da * db + (d % db + hb) % db
            for step in range(p * rows // each, -(-(p + 1) * rows // each)):
                if step not in order:
                    order.append(step)
            done[k] = max(done[k], len(order))
        codes.append(sum(step * steps**t for t, step in enumerate(order)))
    first = -(-rows // 256) * 128
    chunks = []
    for side, (low, high) in enumerate(((0, first), (first, rows))):
        tiles, start = -(-(high - low) // 128), low
        for left in range(min(3, tiles), 0, -1):
            stop = min(high, start + -(-tiles // left) * 128)
            tiles -= -(-tiles // left)
            chunks.append((side, start, start - low, stop - start))
            start = stop
    return (da, db), hops, codes, done, chunks


def slot_count(da, db):
    return (db - 1) * da + (da - 1) * db + da - 1 + db - 1


def results(*refs):
    ins, outs, sems = refs[:4], refs[4:8], refs[8]
    copies = [pltpu.make_async_copy(ins[i], outs[i], sems.at[i]) for i in range(4)]
    for copy in copies:
        copy.start()
    for copy in copies:
        copy.wait()


def kernel(
    sizes,
    fields, cot, w1_hbm, w2_hbm,
    out_ref, fgrad_ref, g1_ref, g2_ref,
    w1, w2, p_f, p_c, p_h, p_g, z_a, z_b, z_c, lhs_f, lhs_h, pre,
    own, send_a, recv_a, recv_b, send_z, recv_z,
    sem_w, sem_f, halo_send, halo_recv, a_send, a_recv, b_send, b_recv, z_send, z_recv,
):
    ndp, npx, npy, rollouts = sizes
    nx, ny, nz, ch = fields.shape
    cells = nx * ny * nz
    half = ch // npy
    kc = own.shape[1]
    rows = kc // ndp
    (da, db), hops, codes, done, chunks = reduction_plan(ndp, kc, 9)
    wid = recv_z[0].shape[2]
    nj = half // wid
    d, x, y = lax.axis_index("dp"), lax.axis_index("px"), lax.axis_index("py")

    inner = pl.ds(1, nx), pl.ds(1, ny)
    load_f = pltpu.make_async_copy(fields, p_f.at[inner], sem_f.at[0])
    load_c = pltpu.make_async_copy(cot, p_c.at[inner], sem_f.at[1])
    def load_w(which, action):
        for n in range(LOADS):
            part = pl.ds(n * (kc // LOADS), kc // LOADS)
            source, target = ((w1_hbm, w1), (w2_hbm, w2))[which]
            copy = pltpu.make_async_copy(source.at[part], target.at[part], sem_w.at[which, n])
            copy.start() if action == "start" else copy.wait()

    load_f.start()
    load_w(0, "start")
    load_c.start()

    barrier = pltpu.get_barrier_semaphore()
    for i in range(1, ndp):
        pl.semaphore_signal(
            barrier, inc=1, device_id=(lax.rem(d + i, ndp), x, y), device_id_type=MESH
        )
    for i in range(1, npx * npy):
        other = lax.rem(x * npy + y + i, npx * npy)
        pl.semaphore_signal(
            barrier, inc=1, device_id=(d, other // npy, lax.rem(other, npy)), device_id_type=MESH
        )
    pl.semaphore_wait(barrier, ndp - 1 + npx * npy - 1)

    def exists(dx, dy):
        return (x + dx >= 0) & (x + dx < npx) & (y + dy >= 0) & (y + dy < npy)

    def span_src(step, size, base):
        if step == 0:
            return pl.ds(base, size)
        return pl.ds(base if step < 0 else base + size - 1, 1)

    def span_dst(step, size):
        if step == 0:
            return pl.ds(1, size)
        return pl.ds(size + 1 if step < 0 else 0, 1)

    def halo_copy(which, src, base, padded, index):
        dx, dy = DIRS[index]
        return pltpu.make_async_remote_copy(
            src_ref=src.at[span_src(dx, nx, base), span_src(dy, ny, base)],
            dst_ref=padded.at[span_dst(dx, nx), span_dst(dy, ny)],
            send_sem=halo_send.at[which, index],
            recv_sem=halo_recv.at[which, index],
            device_id=(d, x + dx, y + dy),
            device_id_type=MESH,
        )

    def halo_start(which, src, base, padded, group):
        for index in group:
            dx, dy = DIRS[index]

            @pl.when(exists(dx, dy))
            def _():
                halo_copy(which, src, base, padded, index).start()

            @pl.when(jnp.logical_not(exists(-dx, -dy)))
            def _():
                sx, sy = span_dst(dx, nx), span_dst(dy, ny)
                padded[sx, sy] = jnp.zeros((sx.size, sy.size, nz, ch), BF16)

    def halo_wait(which, src, base, padded, group):
        for index in group:
            dx, dy = DIRS[index]

            @pl.when(exists(dx, dy))
            def _():
                halo_copy(which, src, base, padded, index).wait_send()

            @pl.when(exists(-dx, -dy))
            def _():
                halo_copy(which, src, base, padded, index).wait_recv()

    def build(padded, shifted, low, high, stride=1):
        @pl.loop(low, high)
        def _(j):
            i = j * stride
            plane = padded[i]
            flat = plane.reshape((ny + 2) * nz, ch).astype(F32)
            place = lax.broadcasted_iota(jnp.int32, flat.shape, 0) % nz
            before = jnp.where(place == 0, 0.0, pltpu.roll(flat, 1, 0))
            after = jnp.where(place == nz - 1, 0.0, pltpu.roll(flat, flat.shape[0] - 1, 0))
            shifted[i, :, :, 0:ch] = before.astype(BF16).reshape(plane.shape)
            shifted[i, :, :, ch : 2 * ch] = plane
            shifted[i, :, :, 2 * ch : 3 * ch] = after.astype(BF16).reshape(plane.shape)

    tile = ny * nz

    def conv(shifted, weight, flipped, finish, inside_first, beside, low=0, high=nx):
        @pl.loop(low, high)
        def _(j):
            for at, task in beside:
                @pl.when(j == at)
                def _():
                    task()

            if inside_first:
                i = jnp.where(j < nx - 2, j + 1, (j - (nx - 2)) * (nx - 1))
            else:
                i = jnp.where(j < 2, j * (nx - 1), j - 1)
            total = None
            for a in range(3):
                for b in range(3):
                    first = (9 * a + 3 * b) * ch
                    if not flipped:
                        lhs = shifted[i + a, pl.ds(b, ny)].reshape(tile, 3 * ch)
                        term = jnp.dot(
                            lhs, weight[pl.ds(first, 3 * ch)], preferred_element_type=F32
                        )
                        total = term if total is None else total + term
                        continue
                    for c in range(3):
                        lhs = shifted[
                            i + 2 - a, pl.ds(2 - b, ny), :, pl.ds((2 - c) * ch, ch)
                        ].reshape(tile, ch)
                        term = lax.dot_general(
                            lhs,
                            weight[pl.ds(first + c * ch, ch)],
                            (((1,), (1,)), ((), ())),
                            preferred_element_type=F32,
                        )
                        total = term if total is None else total + term
            finish(i, total)

    partner = 1 - y

    def a_copy(which, step):
        part = pl.ds(pl.multiple_of(step * 3 * ch, 3 * ch), 3 * ch)
        return pltpu.make_async_remote_copy(
            src_ref=send_a.at[which, part],
            dst_ref=recv_a.at[which, part],
            send_sem=a_send.at[which, step],
            recv_sem=a_recv.at[which, step],
            device_id=(d, x, partner),
            device_id_type=MESH,
        )

    ia, ib = d // db, lax.rem(d, db)
    groups = [[], [], []]
    for side in range(2):
        here = [chunk for chunk in range(len(chunks)) if chunks[chunk][0] == side]
        for order, chunk in enumerate(here):
            groups[order].append(chunk)
    code = jnp.int32(codes[0])
    for i in range(1, ndp):
        code = jnp.where(d == i, jnp.int32(codes[i]), code)

    def ring(index, hop, count):
        return lax.rem(index + hop, count) if hop else index

    def piece(ha, hb, chunk):
        first = (ring(ia, ha, da) * db + ring(ib, hb, db)) * rows + chunks[chunk][1]
        return pl.ds(pl.multiple_of(first, 16), chunks[chunk][3])

    def slot_of(phase, side, ha, hb):
        if phase == 0:
            return (hb - 1) * da + ha if side == 0 else (db - 1) * da + (ha - 1) * db + hb
        base = (db - 1) * da + (da - 1) * db
        return base + ha - 1 if side == 0 else base + da - 1 + hb - 1

    def b_copy(which, phase, ha, hb, chunk):
        side, _, offset, size = chunks[chunk]
        if (side == 0) == (phase == 0):
            peer = ia * db + ring(ib, hb, db)
        else:
            peer = ring(ia, ha, da) * db + ib
        slot = slot_of(phase, side, ha, hb)
        return pltpu.make_async_remote_copy(
            src_ref=send_a.at[which, piece(ha, hb, chunk)],
            dst_ref=recv_b.at[which, slot, pl.ds(offset, size)],
            send_sem=b_send.at[which, slot, chunk],
            recv_sem=b_recv.at[which, slot, chunk],
            device_id=(peer, x, y),
            device_id_type=MESH,
        )

    def arrived(which, phase, ha, hb, chunk):
        side, _, offset, size = chunks[chunk]
        b_copy(which, phase, ha, hb, chunk).wait_recv()
        return recv_b[which, slot_of(phase, side, ha, hb), pl.ds(offset, size)].astype(F32)

    def piece_start(which, k):
        for t in range(done[k - 1] if k else 0, done[k]):
            a_copy(which, lax.rem(code // 9**t, 9)).wait()
        ha, hb = hops[k]
        for chunk, (side, _, _, _) in enumerate(chunks):
            part = piece(ha, hb, chunk)
            total = own[which, part] + recv_a[which, part].astype(F32)
            if (hb if side == 0 else ha) > 0:
                send_a[which, part] = total.astype(BF16)
                if chunk in groups[0] or (ha and hb and chunk in groups[1]):
                    b_copy(which, 0, ha, hb, chunk).start()
            else:
                own[which, part] = total

    def pieces_send(which, diagonal, order):
        for ha, hb in hops:
            if order < len(groups) and (ha > 0 and hb > 0) == diagonal:
                for chunk in groups[order]:
                    if (hb if chunks[chunk][0] == 0 else ha) > 0:
                        b_copy(which, 0, ha, hb, chunk).start()

    after = [-(-(count + LAG) // 3) for count in done]

    def weight_grad(which, lhs, shifted, beside):
        def three(group, left):
            for k in range(len(hops)):
                if after[k] < 3:
                    @pl.when(group == after[k])
                    def _():
                        piece_start(which, k)

            for at, task in beside:
                @pl.when(group == at)
                def _():
                    task()

            steps = []
            for _ in range(3):
                step = lax.rem(left, 9)
                steps.append(step)
                left = left // 9
                a, b = step // 3, lax.rem(step, 3)
                rhs = shifted[pl.ds(2 - a, nx), pl.ds(2 - b, ny)].reshape(cells, 3 * ch)
                prod = jnp.dot(lhs[...], rhs, preferred_element_type=F32)
                for c in range(3):
                    block = prod[:, (2 - c) * ch : (3 - c) * ch]
                    here = pl.ds(pl.multiple_of(step * 3 * ch, ch) + c * ch, ch)
                    low, high = block[:, :half], block[:, half:]
                    own[which, here] = jnp.where(y == 0, low, high)
                    send_a[which, here] = jnp.where(y == 0, high, low).astype(BF16)
            for step in steps:
                a_copy(which, step).start()
            return left

        lax.fori_loop(0, 3, three, code)

    def pieces_rest(which):
        for k in range(len(hops)):
            if after[k] >= 3 and k < len(hops) - 1:
                piece_start(which, k)

    def own_piece(which):
        piece_start(which, len(hops) - 1)

    def advance(which, order):
        for chunk in groups[order]:
            relay(which, chunk)
        pieces_send(which, True, order + 2)
        pieces_send(which, False, order + 1)

    def relay(which, chunk):
        side = chunks[chunk][0]
        for hop in range(1, da if side == 0 else db):
            ha, hb = (hop, 0) if side == 0 else (0, hop)
            part = piece(ha, hb, chunk)
            total = own[which, part]
            for first in range(1, db if side == 0 else da):
                fa, fb = (hop, first) if side == 0 else (first, hop)
                total = total + arrived(which, 0, fa, fb, chunk)
            send_a[which, part] = total.astype(BF16)
            b_copy(which, 1, ha, hb, chunk).start()

    def z_ids(j):
        owner = y * nj + j
        return owner // npy, lax.rem(owner, npy)

    def z_remote(which, j, chunk):
        px_o, py_o = z_ids(j)
        return pltpu.make_async_remote_copy(
            src_ref=send_z[chunk].at[which, pl.ds(j * wid, wid)],
            dst_ref=recv_z[chunk].at[which, x],
            send_sem=z_send.at[which, j, chunk],
            recv_sem=z_recv.at[which, x, chunk],
            device_id=(d, px_o, py_o),
            device_id_type=MESH,
        )

    def columns_start(which, chunk):
        side, _, _, size = chunks[chunk]
        total = own[which, piece(0, 0, chunk)]
        for hop in range(1, db if side == 0 else da):
            total = total + arrived(which, 0, *((0, hop) if side == 0 else (hop, 0)), chunk)
        for hop in range(1, da if side == 0 else db):
            total = total + arrived(which, 1, *((hop, 0) if side == 0 else (0, hop)), chunk)
        pad = -size % 128
        if pad:
            total = jnp.concatenate([total, jnp.zeros((pad, half), F32)], axis=0)
        send_z[chunk][which] = total.T.astype(BF16)
        for j in range(nj):
            px_o, py_o = z_ids(j)
            mine = (px_o == x) & (py_o == y)

            @pl.when(jnp.logical_not(mine))
            def _():
                z_remote(which, j, chunk).start()

            @pl.when(mine)
            def _():
                recv_z[chunk][which, x] = send_z[chunk][which, j * wid : (j + 1) * wid]

    def columns_send(which, order):
        for chunk in groups[order]:
            columns_start(which, chunk)

    def finish_grad(which, grad, chunk):
        total = None
        for i in range(npx):
            here = recv_z[chunk].at[which, i]

            @pl.when((x != i) | (y != (x * npy + y) // nj))
            def _():
                pltpu.make_async_copy(here, here, z_recv.at[which, i, chunk]).wait()

            term = recv_z[chunk][which, i].astype(F32)
            total = term if total is None else total + term
        _, start, _, size = chunks[chunk]
        grad[:, start : start + size] = (total / rollouts)[:, :size]

    def sent(which):
        for chunk, (side, _, _, _) in enumerate(chunks):
            for ha, hb in hops:
                if (hb if side == 0 else ha) > 0:
                    b_copy(which, 0, ha, hb, chunk).wait_send()
            for hop in range(1, da if side == 0 else db):
                b_copy(which, 1, *((hop, 0) if side == 0 else (0, hop)), chunk).wait_send()
            for j in range(nj):
                px_o, py_o = z_ids(j)

                @pl.when(jnp.logical_not((px_o == x) & (py_o == y)))
                def _():
                    z_remote(which, j, chunk).wait_send()

    every = range(len(chunks))

    load_f.wait()
    halo_start(0, p_f, 1, p_f, ACROSS)
    halo_start(0, p_f, 1, p_f, ALONG)
    load_c.wait()
    halo_start(1, p_c, 1, p_c, ACROSS)
    halo_wait(0, p_f, 1, p_f, ACROSS)
    build(p_f, z_a, 1, nx + 1)

    def hidden_finish(i, total):
        pre[i] = total
        value = (total * (0.5 * (1.0 + gelu_parts(total)))).astype(BF16)
        p_h[i + 1, pl.ds(1, ny)] = value.reshape(ny, nz, ch)

    load_w(0, "wait")
    load_w(1, "start")
    def outer_fields():
        halo_start(1, p_c, 1, p_c, ALONG)
        halo_wait(1, p_c, 1, p_c, ACROSS)
        build(p_c, z_b, 1, nx + 1)
        halo_wait(0, p_f, 1, p_f, ALONG)
        build(p_f, z_a, 0, 2, nx + 1)

    conv(z_a, w1, False, hidden_finish, True, [(nx - 2, outer_fields)])
    halo_start(2, p_h, 1, p_h, ALONG)
    halo_start(2, p_h, 1, p_h, ACROSS)
    lhs_h[...] = p_h[pl.ds(1, nx), pl.ds(1, ny)].reshape(cells, ch).T
    halo_wait(1, p_c, 1, p_c, ALONG)
    build(p_c, z_b, 0, 2, nx + 1)
    def grad_finish(i, total):
        v = pre[i]
        t = gelu_parts(v)
        slope = 0.5 * (1.0 + t) + (0.5 * v) * (1.0 - t * t) * (
            GELU_C * (1.0 + (3.0 * GELU_A) * (v * v))
        )
        p_g[i + 1, pl.ds(1, ny)] = (total * slope).astype(BF16).reshape(ny, nz, ch)

    def outer_grad():
        load_w(1, "wait")
        conv(z_b, w2, True, grad_finish, False, [], 0, 2)
        halo_start(3, p_g, 1, p_g, ALONG)

    weight_grad(1, lhs_h, z_b, [(2, outer_grad)])
    pieces_rest(1)
    advance(1, 0)
    conv(z_b, w2, True, grad_finish, False, [], 2, nx)
    halo_start(3, p_g, 1, p_g, ACROSS)
    own_piece(1)
    advance(1, 1)
    lhs_f[...] = p_f[inner].reshape(cells, ch).T
    halo_wait(2, p_h, 1, p_h, ALONG)
    halo_wait(2, p_h, 1, p_h, ACROSS)
    build(p_h, z_a, 0, nx + 2)
    halo_wait(3, p_g, 1, p_g, ACROSS)
    build(p_g, z_c, 1, nx + 1)
    halo_wait(3, p_g, 1, p_g, ALONG)
    build(p_g, z_c, 0, 2, nx + 1)
    weight_grad(
        0, lhs_f, z_c,
        [
            (0, lambda: columns_send(1, 0)),
            (1, lambda: advance(1, 2)),
            (2, lambda: columns_send(1, 1)),
        ],
    )
    pieces_rest(0)

    def out_finish(i, total):
        out_ref[i] = (
            (p_f[i + 1, pl.ds(1, ny)].reshape(tile, ch).astype(F32) + total)
            .astype(BF16)
            .reshape(ny, nz, ch)
        )

    def own_next():
        own_piece(0)
        advance(0, 1)

    conv(z_a, w2, False, out_finish, True, [(1, lambda: advance(0, 0)), (2, own_next), (3, lambda: columns_send(1, 2))])

    def field_finish(i, total):
        fgrad_ref[i] = (
            (p_c[i + 1, pl.ds(1, ny)].reshape(tile, ch).astype(F32) + total)
            .astype(BF16)
            .reshape(ny, nz, ch)
        )

    conv(
        z_c, w1, True, field_finish, True,
        [(1, lambda: columns_send(0, 0)), (3, lambda: advance(0, 2))],
    )
    for chunk in every:
        finish_grad(1, g2_ref, chunk)
    sent(1)
    columns_send(0, 1)
    columns_send(0, 2)
    for chunk in groups[0] + groups[1] + groups[2]:
        finish_grad(0, g1_ref, chunk)
    sent(0)


def body(sizes, fields, cotangent, first_weight, second_weight):
    ndp, npx, npy = sizes
    batch, nx, ny, nz, ch = fields.shape
    kc = first_weight.shape[0]
    half = ch // npy
    (da, db), _, _, _, chunks = reduction_plan(ndp, kc, 9)
    slots = slot_count(da, db)
    longest = max(offset + size for _, _, offset, size in chunks)
    rows = kc // ndp
    widths = [-(-size // 128) * 128 for _, _, _, size in chunks]
    wid = ch // (npx * npy)
    cells = nx * ny * nz
    vmem = pl.BlockSpec(memory_space=pltpu.VMEM)
    hbm = pl.BlockSpec(memory_space=pltpu.HBM)
    anywhere = pl.BlockSpec(memory_space=pl.ANY)
    padded = pltpu.VMEM((nx + 2, ny + 2, nz, ch), BF16)
    shifted = pltpu.VMEM((nx + 2, ny + 2, nz, 3 * ch), BF16)
    dma = pltpu.SemaphoreType.DMA
    block = (nx, ny, nz, ch)
    out, fgrad, g1, g2 = pl.pallas_call(
        functools.partial(kernel, (ndp, npx, npy, batch * ndp)),
        out_shape=(
            jax.ShapeDtypeStruct(block, BF16),
            jax.ShapeDtypeStruct(block, BF16),
            jax.ShapeDtypeStruct((wid, rows), F32),
            jax.ShapeDtypeStruct((wid, rows), F32),
        ),
        in_specs=[hbm] * 4,
        out_specs=(vmem, vmem, vmem, vmem),
        scratch_shapes=[
            pltpu.VMEM((kc, ch), BF16),
            pltpu.VMEM((kc, ch), BF16),
            padded, padded, padded, padded,
            shifted, shifted, shifted,
            pltpu.VMEM((ch, cells), BF16),
            pltpu.VMEM((ch, cells), BF16),
            pltpu.VMEM((nx, ny * nz, ch), F32),
            pltpu.VMEM((2, kc, half), F32),
            pltpu.VMEM((2, kc, half), BF16),
            pltpu.VMEM((2, kc, half), BF16),
            pltpu.VMEM((2, slots, longest, half), BF16),
            [pltpu.VMEM((2, half, width), BF16) for width in widths],
            [pltpu.VMEM((2, npx, wid, width), BF16) for width in widths],
            dma((2, LOADS)), dma((2,)),
            dma((4, 8)), dma((4, 8)),
            dma((2, 9)), dma((2, 9)),
            dma((2, slots, len(chunks))), dma((2, slots, len(chunks))),
            dma((2, half // wid, len(chunks))), dma((2, npx, len(chunks))),
        ],
        compiler_params=pltpu.CompilerParams(
            collective_id=0, has_side_effects=True, vmem_limit_bytes=48000000
        ),
        name="closure",
    )(*(pltpu.with_memory_space_constraint(v, pltpu.HBM) for v in (fields.reshape(block), cotangent.reshape(block), first_weight, second_weight)))
    out, fgrad, g1, g2 = pl.pallas_call(
        results,
        out_shape=(
            jax.ShapeDtypeStruct(block, BF16),
            jax.ShapeDtypeStruct(block, BF16),
            jax.ShapeDtypeStruct((wid, rows), F32),
            jax.ShapeDtypeStruct((wid, rows), F32),
        ),
        in_specs=[anywhere] * 4,
        out_specs=(hbm,) * 4,
        scratch_shapes=[dma((4,))],
        compiler_params=pltpu.CompilerParams(vmem_limit_bytes=1 << 20),
        name="results",
    )(out, fgrad, g1, g2)
    return (
        out.reshape(fields.shape),
        fgrad.reshape(fields.shape),
        g1.T,
        g2.T,
    )


def solution(mesh):
    sizes = tuple(mesh.shape[name] for name in ("dp", "px", "py"))
    placed = (P("dp", "px", "py", None, None), P("dp", "px", "py", None, None), P(), P())
    return jax.shard_map(
        functools.partial(body, sizes),
        mesh=mesh,
        in_specs=placed,
        out_specs=(
            P("dp", "px", "py", None, None),
            P("dp", "px", "py", None, None),
            P("dp", ("px", "py")),
            P("dp", ("px", "py")),
        ),
        check_vma=False,
    )
```

```python
import functools

import jax
import jax.numpy as jnp
from jax import lax
from jax.experimental import pallas as pl
from jax.experimental.pallas import tpu as pltpu
from jax.sharding import PartitionSpec as P

MESH = pl.DeviceIdType.MESH
F32, BF16 = jnp.float32, jnp.bfloat16
DIRS = [(dx, dy) for dx in (-1, 0, 1) for dy in (-1, 0, 1) if dx or dy]
ALONG = [i for i, (dx, _) in enumerate(DIRS) if dx]
ACROSS = [i for i, (dx, _) in enumerate(DIRS) if not dx]
GELU_C = 0.7978845608028654
GELU_A = 0.044715
LAG = 1
LOADS = 4


def gelu_parts(v):
    return jnp.tanh(GELU_C * (v + GELU_A * (v * v * v)))


def reduction_plan(ndp, kc, steps):
    db = 2 if ndp % 2 == 0 else 1
    da = ndp // db
    rows = kc // ndp
    hops = [(ha, hb) for ha in range(1, da) for hb in range(1, db)]
    hops += [(0, hb) for hb in range(1, db)] + [(ha, 0) for ha in range(1, da)] + [(0, 0)]
    each = kc // steps
    codes, done = [], [0] * ndp
    for d in range(ndp):
        order = []
        for k, (ha, hb) in enumerate(hops):
            p = (d // db + ha) % da * db + (d % db + hb) % db
            for step in range(p * rows // each, -(-(p + 1) * rows // each)):
                if step not in order:
                    order.append(step)
            done[k] = max(done[k], len(order))
        codes.append(sum(step * steps**t for t, step in enumerate(order)))
    first = -(-rows // 256) * 128
    chunks = []
    for side, (low, high) in enumerate(((0, first), (first, rows))):
        tiles, start = -(-(high - low) // 128), low
        for left in range(min(3, tiles), 0, -1):
            take = tiles if left == 1 else max(1, min(-(-tiles // 2), tiles - left + 1, 3))
            stop = min(high, start + take * 128)
            tiles -= take
            chunks.append((side, start, start - low, stop - start))
            start = stop
    return (da, db), hops, codes, done, chunks


def slot_count(da, db):
    return (db - 1) * da + (da - 1) * db + da - 1 + db - 1


def results(*refs):
    ins, outs, sems = refs[:4], refs[4:8], refs[8]
    copies = [pltpu.make_async_copy(ins[i], outs[i], sems.at[i]) for i in range(4)]
    for copy in copies:
        copy.start()
    for copy in copies:
        copy.wait()


def kernel(
    sizes,
    fields, cot, w1_hbm, w2_hbm,
    out_ref, fgrad_ref, g1_ref, g2_ref,
    w1, w2, p_f, p_c, p_h, p_g, z_a, z_b, z_c, lhs_f, lhs_h, pre,
    own, send_a, recv_a, recv_b, send_z, recv_z,
    sem_w, sem_f, halo_send, halo_recv, a_send, a_recv, b_send, b_recv, z_send, z_recv,
):
    ndp, npx, npy, rollouts = sizes
    nx, ny, nz, ch = fields.shape
    cells = nx * ny * nz
    half = ch // npy
    kc = own.shape[1]
    rows = kc // ndp
    (da, db), hops, codes, done, chunks = reduction_plan(ndp, kc, 9)
    wid = recv_z[0].shape[2]
    nj = half // wid
    d, x, y = lax.axis_index("dp"), lax.axis_index("px"), lax.axis_index("py")

    inner = pl.ds(1, nx), pl.ds(1, ny)
    load_f = pltpu.make_async_copy(fields, p_f.at[inner], sem_f.at[0])
    load_c = pltpu.make_async_copy(cot, p_c.at[inner], sem_f.at[1])
    def load_w(which, action):
        for n in range(LOADS):
            part = pl.ds(n * (kc // LOADS), kc // LOADS)
            source, target = ((w1_hbm, w1), (w2_hbm, w2))[which]
            copy = pltpu.make_async_copy(source.at[part], target.at[part], sem_w.at[which, n])
            copy.start() if action == "start" else copy.wait()

    load_f.start()
    load_w(0, "start")
    load_c.start()

    barrier = pltpu.get_barrier_semaphore()
    for i in range(1, ndp):
        pl.semaphore_signal(
            barrier, inc=1, device_id=(lax.rem(d + i, ndp), x, y), device_id_type=MESH
        )
    for i in range(1, npx * npy):
        other = lax.rem(x * npy + y + i, npx * npy)
        pl.semaphore_signal(
            barrier, inc=1, device_id=(d, other // npy, lax.rem(other, npy)), device_id_type=MESH
        )
    pl.semaphore_wait(barrier, ndp - 1 + npx * npy - 1)

    def exists(dx, dy):
        return (x + dx >= 0) & (x + dx < npx) & (y + dy >= 0) & (y + dy < npy)

    def span_src(step, size, base):
        if step == 0:
            return pl.ds(base, size)
        return pl.ds(base if step < 0 else base + size - 1, 1)

    def span_dst(step, size):
        if step == 0:
            return pl.ds(1, size)
        return pl.ds(size + 1 if step < 0 else 0, 1)

    def halo_copy(which, src, base, padded, index):
        dx, dy = DIRS[index]
        return pltpu.make_async_remote_copy(
            src_ref=src.at[span_src(dx, nx, base), span_src(dy, ny, base)],
            dst_ref=padded.at[span_dst(dx, nx), span_dst(dy, ny)],
            send_sem=halo_send.at[which, index],
            recv_sem=halo_recv.at[which, index],
            device_id=(d, x + dx, y + dy),
            device_id_type=MESH,
        )

    def halo_start(which, src, base, padded, group):
        for index in group:
            dx, dy = DIRS[index]

            @pl.when(exists(dx, dy))
            def _():
                halo_copy(which, src, base, padded, index).start()

            @pl.when(jnp.logical_not(exists(-dx, -dy)))
            def _():
                sx, sy = span_dst(dx, nx), span_dst(dy, ny)
                padded[sx, sy] = jnp.zeros((sx.size, sy.size, nz, ch), BF16)

    def halo_wait(which, src, base, padded, group):
        for index in group:
            dx, dy = DIRS[index]

            @pl.when(exists(dx, dy))
            def _():
                halo_copy(which, src, base, padded, index).wait_send()

            @pl.when(exists(-dx, -dy))
            def _():
                halo_copy(which, src, base, padded, index).wait_recv()

    def build(padded, shifted, low, high, stride=1):
        @pl.loop(low, high)
        def _(j):
            i = j * stride
            plane = padded[i]
            flat = plane.reshape((ny + 2) * nz, ch).astype(F32)
            place = lax.broadcasted_iota(jnp.int32, flat.shape, 0) % nz
            before = jnp.where(place == 0, 0.0, pltpu.roll(flat, 1, 0))
            after = jnp.where(place == nz - 1, 0.0, pltpu.roll(flat, flat.shape[0] - 1, 0))
            shifted[i, :, :, 0:ch] = before.astype(BF16).reshape(plane.shape)
            shifted[i, :, :, ch : 2 * ch] = plane
            shifted[i, :, :, 2 * ch : 3 * ch] = after.astype(BF16).reshape(plane.shape)

    tile = ny * nz

    def conv(shifted, weight, flipped, finish, inside_first, beside, low=0, high=nx):
        @pl.loop(low, high)
        def _(j):
            for at, task in beside:
                @pl.when(j == at)
                def _():
                    task()

            if inside_first:
                i = jnp.where(j < nx - 2, j + 1, (j - (nx - 2)) * (nx - 1))
            else:
                i = jnp.where(j < 2, j * (nx - 1), j - 1)
            total = None
            for a in range(3):
                for b in range(3):
                    first = (9 * a + 3 * b) * ch
                    if not flipped:
                        lhs = shifted[i + a, pl.ds(b, ny)].reshape(tile, 3 * ch)
                        term = jnp.dot(
                            lhs, weight[pl.ds(first, 3 * ch)], preferred_element_type=F32
                        )
                        total = term if total is None else total + term
                        continue
                    for c in range(3):
                        lhs = shifted[
                            i + 2 - a, pl.ds(2 - b, ny), :, pl.ds((2 - c) * ch, ch)
                        ].reshape(tile, ch)
                        term = lax.dot_general(
                            lhs,
                            weight[pl.ds(first + c * ch, ch)],
                            (((1,), (1,)), ((), ())),
                            preferred_element_type=F32,
                        )
                        total = term if total is None else total + term
            finish(i, total)

    partner = 1 - y

    def a_copy(which, step):
        part = pl.ds(pl.multiple_of(step * 3 * ch, 3 * ch), 3 * ch)
        return pltpu.make_async_remote_copy(
            src_ref=send_a.at[which, part],
            dst_ref=recv_a.at[which, part],
            send_sem=a_send.at[which, step],
            recv_sem=a_recv.at[which, step],
            device_id=(d, x, partner),
            device_id_type=MESH,
        )

    ia, ib = d // db, lax.rem(d, db)
    groups = [[], [], []]
    for side in range(2):
        here = [chunk for chunk in range(len(chunks)) if chunks[chunk][0] == side]
        for order, chunk in enumerate(here):
            groups[order].append(chunk)
    code = jnp.int32(codes[0])
    for i in range(1, ndp):
        code = jnp.where(d == i, jnp.int32(codes[i]), code)

    def ring(index, hop, count):
        return lax.rem(index + hop, count) if hop else index

    def piece(ha, hb, chunk):
        first = (ring(ia, ha, da) * db + ring(ib, hb, db)) * rows + chunks[chunk][1]
        return pl.ds(pl.multiple_of(first, 16), chunks[chunk][3])

    def slot_of(phase, side, ha, hb):
        if phase == 0:
            return (hb - 1) * da + ha if side == 0 else (db - 1) * da + (ha - 1) * db + hb
        base = (db - 1) * da + (da - 1) * db
        return base + ha - 1 if side == 0 else base + da - 1 + hb - 1

    def b_copy(which, phase, ha, hb, chunk):
        side, _, offset, size = chunks[chunk]
        if (side == 0) == (phase == 0):
            peer = ia * db + ring(ib, hb, db)
        else:
            peer = ring(ia, ha, da) * db + ib
        slot = slot_of(phase, side, ha, hb)
        return pltpu.make_async_remote_copy(
            src_ref=send_a.at[which, piece(ha, hb, chunk)],
            dst_ref=recv_b.at[which, slot, pl.ds(offset, size)],
            send_sem=b_send.at[which, slot, chunk],
            recv_sem=b_recv.at[which, slot, chunk],
            device_id=(peer, x, y),
            device_id_type=MESH,
        )

    def arrived(which, phase, ha, hb, chunk):
        side, _, offset, size = chunks[chunk]
        b_copy(which, phase, ha, hb, chunk).wait_recv()
        return recv_b[which, slot_of(phase, side, ha, hb), pl.ds(offset, size)].astype(F32)

    def piece_start(which, k):
        for t in range(done[k - 1] if k else 0, done[k]):
            a_copy(which, lax.rem(code // 9**t, 9)).wait()
        ha, hb = hops[k]
        for chunk, (side, _, _, _) in enumerate(chunks):
            part = piece(ha, hb, chunk)
            total = own[which, part] + recv_a[which, part].astype(F32)
            if (hb if side == 0 else ha) > 0:
                send_a[which, part] = total.astype(BF16)
                if chunk in groups[0] or (ha and hb and chunk in groups[1]):
                    b_copy(which, 0, ha, hb, chunk).start()
            else:
                own[which, part] = total

    def pieces_send(which, diagonal, order):
        for ha, hb in hops:
            if order < len(groups) and (ha > 0 and hb > 0) == diagonal:
                for chunk in groups[order]:
                    if (hb if chunks[chunk][0] == 0 else ha) > 0:
                        b_copy(which, 0, ha, hb, chunk).start()

    after = [-(-(count + LAG) // 3) for count in done]

    def weight_grad(which, lhs, shifted, beside):
        def three(group, left):
            for k in range(len(hops)):
                if after[k] < 3:
                    @pl.when(group == after[k])
                    def _():
                        piece_start(which, k)

            for at, task in beside:
                @pl.when(group == at)
                def _():
                    task()

            steps = []
            for _ in range(3):
                step = lax.rem(left, 9)
                steps.append(step)
                left = left // 9
                a, b = step // 3, lax.rem(step, 3)
                rhs = shifted[pl.ds(2 - a, nx), pl.ds(2 - b, ny)].reshape(cells, 3 * ch)
                prod = jnp.dot(lhs[...], rhs, preferred_element_type=F32)
                for c in range(3):
                    block = prod[:, (2 - c) * ch : (3 - c) * ch]
                    here = pl.ds(pl.multiple_of(step * 3 * ch, ch) + c * ch, ch)
                    low, high = block[:, :half], block[:, half:]
                    own[which, here] = jnp.where(y == 0, low, high)
                    send_a[which, here] = jnp.where(y == 0, high, low).astype(BF16)
            for step in steps:
                a_copy(which, step).start()
            return left

        lax.fori_loop(0, 3, three, code)

    def pieces_rest(which):
        for k in range(len(hops)):
            if after[k] >= 3 and k < len(hops) - 1:
                piece_start(which, k)

    def own_piece(which):
        piece_start(which, len(hops) - 1)

    def advance(which, order):
        for chunk in groups[order]:
            relay(which, chunk)
        pieces_send(which, True, order + 2)
        pieces_send(which, False, order + 1)

    def relay(which, chunk):
        side = chunks[chunk][0]
        for hop in range(1, da if side == 0 else db):
            ha, hb = (hop, 0) if side == 0 else (0, hop)
            part = piece(ha, hb, chunk)
            total = own[which, part]
            for first in range(1, db if side == 0 else da):
                fa, fb = (hop, first) if side == 0 else (first, hop)
                total = total + arrived(which, 0, fa, fb, chunk)
            send_a[which, part] = total.astype(BF16)
            b_copy(which, 1, ha, hb, chunk).start()

    def z_ids(j):
        owner = y * nj + j
        return owner // npy, lax.rem(owner, npy)

    def z_remote(which, j, chunk):
        px_o, py_o = z_ids(j)
        return pltpu.make_async_remote_copy(
            src_ref=send_z[chunk].at[which, pl.ds(j * wid, wid)],
            dst_ref=recv_z[chunk].at[which, x],
            send_sem=z_send.at[which, j, chunk],
            recv_sem=z_recv.at[which, x, chunk],
            device_id=(d, px_o, py_o),
            device_id_type=MESH,
        )

    def columns_start(which, chunk):
        side, _, _, size = chunks[chunk]
        total = own[which, piece(0, 0, chunk)]
        for hop in range(1, db if side == 0 else da):
            total = total + arrived(which, 0, *((0, hop) if side == 0 else (hop, 0)), chunk)
        for hop in range(1, da if side == 0 else db):
            total = total + arrived(which, 1, *((hop, 0) if side == 0 else (0, hop)), chunk)
        pad = -size % 128
        if pad:
            total = jnp.concatenate([total, jnp.zeros((pad, half), F32)], axis=0)
        send_z[chunk][which] = total.T.astype(BF16)
        for j in range(nj):
            px_o, py_o = z_ids(j)
            mine = (px_o == x) & (py_o == y)

            @pl.when(jnp.logical_not(mine))
            def _():
                z_remote(which, j, chunk).start()

            @pl.when(mine)
            def _():
                recv_z[chunk][which, x] = send_z[chunk][which, j * wid : (j + 1) * wid]

    def columns_send(which, order):
        for chunk in groups[order]:
            columns_start(which, chunk)

    def finish_grad(which, grad, chunk):
        total = None
        for i in range(npx):
            here = recv_z[chunk].at[which, i]

            @pl.when((x != i) | (y != (x * npy + y) // nj))
            def _():
                pltpu.make_async_copy(here, here, z_recv.at[which, i, chunk]).wait()

            term = recv_z[chunk][which, i].astype(F32)
            total = term if total is None else total + term
        _, start, _, size = chunks[chunk]
        grad[:, start : start + size] = (total / rollouts)[:, :size]

    def sent(which):
        for chunk, (side, _, _, _) in enumerate(chunks):
            for ha, hb in hops:
                if (hb if side == 0 else ha) > 0:
                    b_copy(which, 0, ha, hb, chunk).wait_send()
            for hop in range(1, da if side == 0 else db):
                b_copy(which, 1, *((hop, 0) if side == 0 else (0, hop)), chunk).wait_send()
            for j in range(nj):
                px_o, py_o = z_ids(j)

                @pl.when(jnp.logical_not((px_o == x) & (py_o == y)))
                def _():
                    z_remote(which, j, chunk).wait_send()

    every = range(len(chunks))

    load_f.wait()
    halo_start(0, p_f, 1, p_f, ACROSS)
    halo_start(0, p_f, 1, p_f, ALONG)
    load_c.wait()
    halo_start(1, p_c, 1, p_c, ACROSS)
    halo_wait(0, p_f, 1, p_f, ACROSS)
    build(p_f, z_a, 1, nx + 1)

    def hidden_finish(i, total):
        pre[i] = total
        value = (total * (0.5 * (1.0 + gelu_parts(total)))).astype(BF16)
        p_h[i + 1, pl.ds(1, ny)] = value.reshape(ny, nz, ch)

    load_w(0, "wait")
    load_w(1, "start")
    def outer_fields():
        halo_start(1, p_c, 1, p_c, ALONG)
        halo_wait(1, p_c, 1, p_c, ACROSS)
        build(p_c, z_b, 1, nx + 1)
        halo_wait(0, p_f, 1, p_f, ALONG)
        build(p_f, z_a, 0, 2, nx + 1)

    conv(z_a, w1, False, hidden_finish, True, [(nx - 2, outer_fields)])
    halo_start(2, p_h, 1, p_h, ALONG)
    halo_start(2, p_h, 1, p_h, ACROSS)
    lhs_h[...] = p_h[pl.ds(1, nx), pl.ds(1, ny)].reshape(cells, ch).T
    halo_wait(1, p_c, 1, p_c, ALONG)
    build(p_c, z_b, 0, 2, nx + 1)
    def grad_finish(i, total):
        v = pre[i]
        t = gelu_parts(v)
        slope = 0.5 * (1.0 + t) + (0.5 * v) * (1.0 - t * t) * (
            GELU_C * (1.0 + (3.0 * GELU_A) * (v * v))
        )
        p_g[i + 1, pl.ds(1, ny)] = (total * slope).astype(BF16).reshape(ny, nz, ch)

    def outer_grad():
        load_w(1, "wait")
        conv(z_b, w2, True, grad_finish, False, [], 0, 2)
        halo_start(3, p_g, 1, p_g, ALONG)

    weight_grad(1, lhs_h, z_b, [(2, outer_grad)])
    pieces_rest(1)
    advance(1, 0)
    conv(z_b, w2, True, grad_finish, False, [], 2, nx)
    halo_start(3, p_g, 1, p_g, ACROSS)
    own_piece(1)
    advance(1, 1)
    lhs_f[...] = p_f[inner].reshape(cells, ch).T
    halo_wait(2, p_h, 1, p_h, ALONG)
    halo_wait(2, p_h, 1, p_h, ACROSS)
    build(p_h, z_a, 0, nx + 2)
    halo_wait(3, p_g, 1, p_g, ACROSS)
    build(p_g, z_c, 1, nx + 1)
    halo_wait(3, p_g, 1, p_g, ALONG)
    build(p_g, z_c, 0, 2, nx + 1)
    weight_grad(
        0, lhs_f, z_c,
        [
            (0, lambda: columns_send(1, 0)),
            (1, lambda: advance(1, 2)),
            (2, lambda: columns_send(1, 1)),
        ],
    )
    pieces_rest(0)

    def out_finish(i, total):
        out_ref[i] = (
            (p_f[i + 1, pl.ds(1, ny)].reshape(tile, ch).astype(F32) + total)
            .astype(BF16)
            .reshape(ny, nz, ch)
        )

    def own_next():
        own_piece(0)
        advance(0, 1)

    conv(z_a, w2, False, out_finish, True, [(1, lambda: advance(0, 0)), (2, own_next), (3, lambda: columns_send(1, 2))])

    def field_finish(i, total):
        fgrad_ref[i] = (
            (p_c[i + 1, pl.ds(1, ny)].reshape(tile, ch).astype(F32) + total)
            .astype(BF16)
            .reshape(ny, nz, ch)
        )

    conv(
        z_c, w1, True, field_finish, True,
        [(1, lambda: columns_send(0, 0)), (3, lambda: advance(0, 2))],
    )
    for chunk in every:
        finish_grad(1, g2_ref, chunk)
    sent(1)
    columns_send(0, 1)
    columns_send(0, 2)
    for chunk in groups[0] + groups[1] + groups[2]:
        finish_grad(0, g1_ref, chunk)
    sent(0)


def body(sizes, fields, cotangent, first_weight, second_weight):
    ndp, npx, npy = sizes
    batch, nx, ny, nz, ch = fields.shape
    kc = first_weight.shape[0]
    half = ch // npy
    (da, db), _, _, _, chunks = reduction_plan(ndp, kc, 9)
    slots = slot_count(da, db)
    longest = max(offset + size for _, _, offset, size in chunks)
    rows = kc // ndp
    widths = [-(-size // 128) * 128 for _, _, _, size in chunks]
    wid = ch // (npx * npy)
    cells = nx * ny * nz
    vmem = pl.BlockSpec(memory_space=pltpu.VMEM)
    hbm = pl.BlockSpec(memory_space=pltpu.HBM)
    anywhere = pl.BlockSpec(memory_space=pl.ANY)
    padded = pltpu.VMEM((nx + 2, ny + 2, nz, ch), BF16)
    shifted = pltpu.VMEM((nx + 2, ny + 2, nz, 3 * ch), BF16)
    dma = pltpu.SemaphoreType.DMA
    block = (nx, ny, nz, ch)
    out, fgrad, g1, g2 = pl.pallas_call(
        functools.partial(kernel, (ndp, npx, npy, batch * ndp)),
        out_shape=(
            jax.ShapeDtypeStruct(block, BF16),
            jax.ShapeDtypeStruct(block, BF16),
            jax.ShapeDtypeStruct((wid, rows), F32),
            jax.ShapeDtypeStruct((wid, rows), F32),
        ),
        in_specs=[hbm] * 4,
        out_specs=(vmem, vmem, vmem, vmem),
        scratch_shapes=[
            pltpu.VMEM((kc, ch), BF16),
            pltpu.VMEM((kc, ch), BF16),
            padded, padded, padded, padded,
            shifted, shifted, shifted,
            pltpu.VMEM((ch, cells), BF16),
            pltpu.VMEM((ch, cells), BF16),
            pltpu.VMEM((nx, ny * nz, ch), F32),
            pltpu.VMEM((2, kc, half), F32),
            pltpu.VMEM((2, kc, half), BF16),
            pltpu.VMEM((2, kc, half), BF16),
            pltpu.VMEM((2, slots, longest, half), BF16),
            [pltpu.VMEM((2, half, width), BF16) for width in widths],
            [pltpu.VMEM((2, npx, wid, width), BF16) for width in widths],
            dma((2, LOADS)), dma((2,)),
            dma((4, 8)), dma((4, 8)),
            dma((2, 9)), dma((2, 9)),
            dma((2, slots, len(chunks))), dma((2, slots, len(chunks))),
            dma((2, half // wid, len(chunks))), dma((2, npx, len(chunks))),
        ],
        compiler_params=pltpu.CompilerParams(
            collective_id=0, has_side_effects=True, vmem_limit_bytes=48000000
        ),
        name="closure",
    )(*(pltpu.with_memory_space_constraint(v, pltpu.HBM) for v in (fields.reshape(block), cotangent.reshape(block), first_weight, second_weight)))
    out, fgrad, g1, g2 = pl.pallas_call(
        results,
        out_shape=(
            jax.ShapeDtypeStruct(block, BF16),
            jax.ShapeDtypeStruct(block, BF16),
            jax.ShapeDtypeStruct((wid, rows), F32),
            jax.ShapeDtypeStruct((wid, rows), F32),
        ),
        in_specs=[anywhere] * 4,
        out_specs=(hbm,) * 4,
        scratch_shapes=[dma((4,))],
        compiler_params=pltpu.CompilerParams(vmem_limit_bytes=1 << 20),
        name="results",
    )(out, fgrad, g1, g2)
    return (
        out.reshape(fields.shape),
        fgrad.reshape(fields.shape),
        g1.T,
        g2.T,
    )


def solution(mesh):
    sizes = tuple(mesh.shape[name] for name in ("dp", "px", "py"))
    placed = (P("dp", "px", "py", None, None), P("dp", "px", "py", None, None), P(), P())
    return jax.shard_map(
        functools.partial(body, sizes),
        mesh=mesh,
        in_specs=placed,
        out_specs=(
            P("dp", "px", "py", None, None),
            P("dp", "px", "py", None, None),
            P("dp", ("px", "py")),
            P("dp", ("px", "py")),
        ),
        check_vma=False,
    )
```
